32 devices in a mesh: replica: 2 (over y), sky: 4 (over z), freq: 4 (over x, core).
Axes of the slice: x: 2, y: 2, z: 4, core: 2. Of those that a mesh axis runs over, the one named last changes fastest.
Arguments:
- lightcone: bfloat16 [128, 32, 8, 128], P(('replica', 'freq'), None, 'sky'), parts along dimension 0, may hold values from -6 to 6
- cotangent: bfloat16 [128, 32, 8, 128], P(('replica', 'freq'), None, 'sky'), parts along dimension 0, may hold values from -6 to 6
- conv_weight: bfloat16 [32, 288], replicated, may hold values from -0.375 to 0.375
- in_proj: float32 [32, 16], replicated, may hold values from -1 to 1
- out_proj: float32 [32, 16], replicated, may hold values from -0.5 to 0.5
- skip_gain: float32 [32], replicated, may hold values from -4 to 4
- decay: float32 [64, 512], P('freq'), may hold values from 0.4 to 1
Outputs:
- d_lightcone: bfloat16 [128, 32, 8, 128], P(('replica', 'freq'), None, 'sky'), parts along dimension 0
- d_conv: float32 [64, 288], P('replica'), parts along dimension 0
- d_in_proj: float32 [64, 16], P('replica'), parts along dimension 0
- d_out_proj: float32 [64, 16], P('replica'), parts along dimension 0
- d_skip: float32 [64], P('replica'), parts along dimension 0
The draws below stay inside these ranges and needn't reach their ends.
There are 2 independent parts, one for each index of `replica`. The reference program is written for one: setup_inputs(seed, part) draws one part's arguments, and reference() takes and returns one part's arrays. A program takes and returns all parts, laid end to end along the dimension named above; an argument that names none is the same for every part. Nothing has to cross between parts.
All inputs are finite; a program needn't handle non-finite values.
Results may differ from the reference program's by a relative error of at most 0.0055.
Values may be sent and summed in bfloat16 or wider, within the bound.
A program may use at most 128 MiB of HBM per device.

```python
import jax
import jax.numpy as jnp
from jax import lax

C = 32
N = 16
W = 128
SPECTRAL_BINS = 64
H = 8


def draw_decay(key, part):
    subkeys = jax.random.split(key, 6)
    channels = C * N
    fast_mask = jax.random.uniform(subkeys[0], (channels,)) < 0.5
    span_len = jnp.exp(jax.random.uniform(subkeys[1], (channels,), minval=jnp.log(10.0), maxval=jnp.log(40.0)))
    kept_share = jax.random.uniform(subkeys[2], (channels,), minval=0.4, maxval=0.95)
    attenuation_speed = jnp.where(fast_mask, 1.0 / span_len, -jnp.log(kept_share) / SPECTRAL_BINS)
    stochastic_perturbation = jax.random.uniform(subkeys[3], (SPECTRAL_BINS, channels), minval=0.5, maxval=1.5)
    position_sequence = jax.random.randint(subkeys[4], (3,), 0, SPECTRAL_BINS)
    spike_occurrences = jnp.any(jnp.arange(SPECTRAL_BINS)[:, None] == position_sequence[None, :], axis=1)
    reduction_multiplier = jax.random.uniform(subkeys[5], (SPECTRAL_BINS, channels), minval=0.55, maxval=0.85)
    numeric_elements = jnp.exp(-attenuation_speed[None, :] * stochastic_perturbation) * jnp.where(spike_occurrences[:, None], reduction_multiplier, 1.0)
    return numeric_elements.astype(jnp.float32)


def steps_of(rng, dims, pieces, low, top_value):
    level, own = 1.0, jax.random.fold_in(rng, 6)
    for axis_at, shards_of in pieces:
        steps = jnp.exp(jax.random.uniform(jax.random.fold_in(own, axis_at), (shards_of,), jnp.float32, low / len(pieces), top_value / len(pieces)))
        level = level * jnp.repeat(steps, dims[axis_at] // shards_of).reshape([-1 if axis == axis_at else 1 for axis in range(len(dims))])
    return level


def gaussian(own_key, shape, spread, bound, shards=(), kind=jnp.bfloat16):
    factor_of = steps_of(own_key, shape, shards, -0.22, 0.18) if shards else 1.0
    values = jax.random.normal(own_key, shape, jnp.float32) * spread * factor_of
    return jnp.minimum(jnp.maximum(values, -bound), bound).astype(kind)


def setup_inputs(seed: int = 0, part: int = 0) -> dict:
    streams_of = jax.random.split(jax.random.key(seed), 8)
    part_splits = jax.random.split(jax.random.fold_in(streams_of[7], part), 8)
    lightcone = gaussian(part_splits[0], (SPECTRAL_BINS, C, H, W), 1.0, 6.0, ((0, 4), (2, 4)))
    cotangent = gaussian(part_splits[1], (SPECTRAL_BINS, C, H, W), 1.0, 6.0, ((0, 4), (2, 4)))
    conv_weight = gaussian(streams_of[2], (C, 9 * C), (9 * C) ** -0.5, 0.375)
    in_proj = gaussian(streams_of[3], (C, N), 0.2, 1.0, (), jnp.float32)
    out_proj = gaussian(streams_of[4], (C, N), 0.1, 0.5, (), jnp.float32)
    skip_gain = gaussian(streams_of[5], (C,), 1.0, 4.0, (), jnp.float32)
    decay = draw_decay(jax.random.fold_in(streams_of[7], 71), part)
    return dict(lightcone=lightcone, cotangent=cotangent, conv_weight=conv_weight, in_proj=in_proj, out_proj=out_proj, skip_gain=skip_gain, decay=decay)


def shifted_stack(numeric_elements):
    tap_list = []
    for row_off in (-1, 0, 1):
        for col_off in (-1, 0, 1):
            tap_list.append(jnp.roll(numeric_elements, (-row_off, -col_off), axis=(1, 2)))
    return jnp.concatenate(tap_list, axis=0)


def back_stack(numeric_elements):
    tap_list = []
    for row_off in (-1, 0, 1):
        for col_off in (-1, 0, 1):
            tap_list.append(jnp.roll(numeric_elements, (row_off, col_off), axis=(1, 2)))
    return jnp.concatenate(tap_list, axis=0)


def reference(lightcone, cotangent, conv_weight, in_proj, out_proj, skip_gain, decay):
    grad_scale = 1.0 / float(SPECTRAL_BINS * H * W) ** 0.5
    flip_weight = conv_weight.reshape(C, 9, C).transpose(2, 1, 0).reshape(C, 9 * C)

    def forward_conv(frame):
        stacked = shifted_stack(frame).reshape(9 * C, H * W)
        return jnp.dot(conv_weight, stacked, preferred_element_type=jnp.float32).astype(jnp.bfloat16)

    inputs = lax.map(forward_conv, lightcone)
    rates = decay.reshape(SPECTRAL_BINS, C, N)
    cot_flat = cotangent.reshape(SPECTRAL_BINS, C, H * W)

    def fwd_step(carry, slices):
        state, grad_out = carry
        rate_f, input_f, cot_f = slices
        state = rate_f[:, :, None] * state + in_proj[:, :, None] * input_f.astype(jnp.float32)[:, None, :]
        grad_out = grad_out + jnp.sum(cot_f.astype(jnp.float32)[:, None, :] * state, axis=2)
        return (state, grad_out), None

    start = (jnp.zeros((C, N, H * W), jnp.float32), jnp.zeros((C, N), jnp.float32))
    (last_state, grad_out), _ = lax.scan(fwd_step, start, (rates, inputs, cot_flat))

    def back_step(carry, slices):
        later, grad_in = carry
        rate_f, input_f, cot_f = slices
        cot_wide = cot_f.astype(jnp.float32)
        adjoint = out_proj[:, :, None] * cot_wide[:, None, :] + later
        grad_in = grad_in + jnp.sum(adjoint * input_f.astype(jnp.float32)[:, None, :], axis=2)
        d_input = (jnp.sum(in_proj[:, :, None] * adjoint, axis=1) + skip_gain[:, None] * cot_wide).astype(jnp.bfloat16)
        return (rate_f[:, :, None] * adjoint, grad_in), d_input

    (later_end, grad_in), d_inputs = lax.scan(back_step, start, (rates, inputs, cot_flat), reverse=True)
    d_skip = jnp.sum(cot_flat.astype(jnp.float32) * inputs.astype(jnp.float32), axis=(0, 2))

    def back_conv(carry, slices):
        frame, d_frame = slices
        d_grid = d_frame.reshape(C, H, W)
        d_light = jnp.dot(flip_weight, back_stack(d_grid).reshape(9 * C, H * W), preferred_element_type=jnp.float32).astype(jnp.bfloat16)
        stacked = shifted_stack(frame).reshape(9 * C, H * W)
        carry = carry + jnp.dot(d_frame, stacked.T, preferred_element_type=jnp.float32)
        return carry, d_light.reshape(C, H, W)

    grad_conv, d_lightcone = lax.scan(back_conv, jnp.zeros((C, 9 * C), jnp.float32), (lightcone, d_inputs))
    return (d_lightcone, grad_conv * grad_scale, grad_in * grad_scale, grad_out * grad_scale, d_skip * grad_scale)
```

```python
import functools

import jax
import jax.numpy as jnp
from jax import lax
from jax.experimental import pallas as pl
from jax.experimental.pallas import tpu as pltpu
from jax.sharding import PartitionSpec as P

MESH = pl.DeviceIdType.MESH
BF = jnp.bfloat16
F32 = jnp.float32


def dot(a, b):
    return jnp.dot(a, b, preferred_element_type=F32)


def dot_nt(a, b):
    return lax.dot_general(a, b, (((1,), (1,)), ((), ())), preferred_element_type=F32)


def iota(shape, dim):
    return lax.broadcasted_iota(jnp.int32, shape, dim)


def kernel(nf, ns, x_ref, cot_ref, a_ref, b_ref, io_ref, skip_ref, dec_ref,
           dl_ref, pay_out,
           xr, cg, dg, inp, acc, p4, cur, k4, m4, kb, dr, tacc, pay, rs, sk, own,
           halo_s, halo_r, dhalo_s, dhalo_r, dec_s, dec_r, cot_s, cot_r, fwd_s,
           rs_s, rs_r, sk_s, sk_r, ag_s, ag_r):
    F = x_ref.shape[0]
    me = lax.axis_index("freq")
    sky = lax.axis_index("sky")
    core = lax.rem(me, 2)
    chip = me // 2
    chips = nf // 2
    sibling = me + 1 - 2 * core
    nxt = lax.rem(sky + 1, ns)
    prv = lax.rem(sky + ns - 1, ns)
    rows = pay.shape[0] // nf

    barrier = pltpu.get_barrier_semaphore()
    for d in range(1, nf):
        pl.semaphore_signal(barrier, inc=1, device_id={"freq": lax.rem(me + d, nf)}, device_id_type=MESH)
    for d in range(1, ns):
        pl.semaphore_signal(barrier, inc=1, device_id={"sky": lax.rem(sky + d, ns)}, device_id_type=MESH)

    pr, pc = iota((64, 64), 0), iota((64, 64), 1)
    perm = (pc == 2 * lax.rem(pr, 32) + pr // 32).astype(F32).astype(BF)
    for f in range(F):
        xr[f, 32:96, :] = dot(perm, x_ref[f]).astype(BF)
    for f in range(F):
        c2 = dot(perm, cot_ref[f]).astype(BF)
        cg[me, f * 32:(f + 1) * 32, 0:128] = c2[0:32]
        cg[me, f * 32:(f + 1) * 32, 128:256] = c2[32:64]
    dg[me] = dec_ref[...]
    pl.semaphore_wait(barrier, nf + ns - 2)

    def remote(src, dst, s, r, **where):
        return pltpu.make_async_remote_copy(
            src_ref=src, dst_ref=dst, send_sem=s, recv_sem=r, device_id=dict(where), device_id_type=MESH)

    def dec_copy(d):
        return remote(dg.at[me], dg.at[me], dec_s.at[d], dec_r.at[me], freq=jnp.maximum(me - d, 0))

    def cot_copy(d):
        target = jnp.maximum(chip - d, 0) * 2 + core
        return remote(cg.at[me], cg.at[me], cot_s.at[d], cot_r.at[me], freq=target)

    sib_copy = remote(cg.at[me], cg.at[me], cot_s.at[0], cot_r.at[me], freq=sibling)

    def fwd_copy(d):
        slot = jnp.minimum(chip + d, chips - 1) * 2 + core
        return remote(cg.at[slot], cg.at[slot], fwd_s.at[d], cot_r.at[slot], freq=sibling)

    up = remote(xr.at[:, 64:96], xr.at[:, 0:32], halo_s.at[0], halo_r.at[0], sky=nxt)
    down = remote(xr.at[:, 32:64], xr.at[:, 96:128], halo_s.at[1], halo_r.at[1], sky=prv)
    up.start()
    down.start()
    for d in range(1, nf):
        @pl.when(me >= d)
        def _():
            dec_copy(d).start()
    for d in range(1, chips):
        @pl.when(chip >= d)
        def _():
            cot_copy(d).start()

    @pl.when(core == 1)
    def _():
        sib_copy.start()

    sr, sc = iota((128, 256), 0), iota((128, 256), 1)
    shift = jnp.logical_or(lax.rem(sr + 1, 128) == sc, lax.rem(sr + 127, 128) == sc - 128)
    shift = shift.astype(F32).astype(BF)
    er = (iota((128, 2048), 1) // 16 == iota((128, 2048), 0)).astype(F32).astype(BF)
    et = (iota((2048, 128), 0) // 16 == iota((2048, 128), 1)).astype(F32).astype(BF)
    fi = iota((F, 512), 0)
    same = lax.rem(iota((32, 512), 1), 32) == iota((32, 512), 0)
    r64, l64 = iota((64, 128), 0), iota((64, 128), 1)
    diag = lax.rem(r64, 16) == 4 * (r64 // 16) + l64 // 32

    acc[...] = jnp.zeros_like(acc)
    tacc[...] = jnp.zeros_like(tacc)
    cur[...] = jnp.zeros_like(cur)

    up.wait_recv()
    down.wait_recv()
    for f in range(F):
        x = xr[f]
        rolled = dot(x, shift).astype(BF)
        full = jnp.concatenate([rolled[:, 0:128], x, rolled[:, 128:256]], axis=0)
        got = dot(a_ref[...], full).astype(BF)
        inp[f * 32:(f + 1) * 32, 0:128] = got[0:32]
        inp[f * 32:(f + 1) * 32, 128:256] = got[32:64]

    def block(d, carry):
        q = me + d

        @pl.when(d > 0)
        def _():
            pltpu.make_async_remote_copy(
                src_ref=dg.at[q], dst_ref=dg.at[q], send_sem=dec_s.at[0], recv_sem=dec_r.at[q],
                device_id={"freq": sibling}, device_id_type=MESH).wait_recv()

        v = cur[...]
        for g in range(F):
            v = jnp.where(fi == g - F * d, 1.0, v * dg[q, g:g + 1, :])
            G, j = g // 4, g % 4
            p4[G * 16:(G + 1) * 16, j * 512:(j + 1) * 512] = v
        cur[...] = v
        k = dot((p4[...] * io_ref[...]).astype(BF), et)
        k4[...] = k + jnp.where(jnp.logical_and(diag, d == 0), skip_ref[...], 0.0)
        for f in range(F):
            for G in range(4):
                row = jnp.broadcast_to(k4[G * 16 + f:G * 16 + f + 1, :], (32, 128))
                kb[f * 32:(f + 1) * 32, G * 128:(G + 1) * 128] = jnp.where(same[:, 0:128], row, 0.0).astype(BF)

        @pl.when(jnp.logical_and(d > 0, lax.rem(q, 2) == 0))
        def _():
            slot = q + core
            pltpu.make_async_remote_copy(
                src_ref=cg.at[slot], dst_ref=cg.at[slot], send_sem=fwd_s.at[0], recv_sem=cot_r.at[slot],
                device_id={"freq": sibling}, device_id_type=MESH).wait_recv()
            away = q // 2 - chip
            remote(cg.at[slot], cg.at[slot], fwd_s.at[away], cot_r.at[slot], freq=sibling).start()

        @pl.when(jnp.logical_and(d > 0, lax.rem(q, 2) != core))
        def _():
            pltpu.make_async_remote_copy(
                src_ref=cg.at[q], dst_ref=cg.at[q], send_sem=fwd_s.at[0], recv_sem=cot_r.at[q],
                device_id={"freq": sibling}, device_id_type=MESH).wait_recv()

        acc[...] += dot(kb[...], cg[q])
        gram = dot_nt(inp[...], cg[q])
        for f in range(F):
            row = jnp.sum(jnp.where(same, gram[f * 32:(f + 1) * 32, :], 0.0), axis=0, keepdims=True)
            for G in range(4):
                m4[G * 16 + f:G * 16 + f + 1, :] = row[:, G * 128:(G + 1) * 128]

        @pl.when(d == 0)
        def _():
            pay[96:128, :] = jnp.zeros((32, 128), F32)
            pay[100:101, :] = jnp.sum(jnp.where(diag, m4[...], 0.0), axis=0, keepdims=True)

        wide = dot(m4[...].astype(BF), er) * p4[...]
        tacc[...] += jnp.sum(wide.reshape(8, 8, 2048), axis=0)
        return carry

    lax.fori_loop(0, nf - me, block, 0)

    for f in range(F):
        dr[f, 32:64, :] = acc[f * 32:(f + 1) * 32, 0:128].astype(BF)
        dr[f, 64:96, :] = acc[f * 32:(f + 1) * 32, 128:256].astype(BF)
    dup = remote(dr.at[:, 64:96], dr.at[:, 0:32], dhalo_s.at[0], dhalo_r.at[0], sky=nxt)
    ddown = remote(dr.at[:, 32:64], dr.at[:, 96:128], dhalo_s.at[1], dhalo_r.at[1], sky=prv)
    dup.start()
    ddown.start()

    grad = jnp.zeros((192, 128), F32)
    for f in range(F):
        mid = dr[f, 32:96, :]
        rolled = dot(mid, shift).astype(BF)
        full = jnp.concatenate([rolled[:, 128:256], mid, rolled[:, 0:128]], axis=0)
        grad = grad + dot_nt(full, xr[f])
    for k in range(3):
        top = grad[k * 64:k * 64 + 32, 0:96]
        low = grad[k * 64 + 32:k * 64 + 64, 32:128]
        pay[k * 32:(k + 1) * 32, 0:96] = top + low
        pay[k * 32:(k + 1) * 32, 96:128] = jnp.zeros((32, 32), F32)
    t = jnp.sum(tacc[...], axis=0, keepdims=True)
    t = t[:, 0:512] + t[:, 512:1024] + t[:, 1024:1536] + t[:, 1536:2048]
    for k in range(4):
        pay[96 + k:97 + k, :] = t[:, k * 128:(k + 1) * 128]

    def part(ref, i):
        return ref.at[pl.ds(pl.multiple_of(i * rows, 8), rows)]

    def rs_copy(d):
        to = lax.rem(me + d, nf)
        return remote(part(pay, to), rs.at[d], rs_s.at[d], rs_r.at[d], freq=to)

    def sk_copy(d):
        return remote(own, sk.at[d], sk_s.at[d], sk_r.at[d], sky=lax.rem(sky + d, ns))

    def ag_copy(d):
        return remote(part(pay_out, me), part(pay_out, me), ag_s.at[d], ag_r.at[me],
                      freq=lax.rem(me + d, nf))

    def ag_wait(d):
        q = lax.rem(me + nf - d, nf)
        pltpu.make_async_remote_copy(
            src_ref=part(pay_out, q), dst_ref=part(pay_out, q), send_sem=ag_s.at[0], recv_sem=ag_r.at[q],
            device_id={"freq": q}, device_id_type=MESH).wait_recv()

    def light(f):
        x = dr[f]
        rolled = dot(x, shift).astype(BF)
        full = jnp.concatenate([rolled[:, 128:256], x, rolled[:, 0:128]], axis=0)
        dl_ref[f] = dot(b_ref[...], full).astype(BF)

    for d in range(1, nf):
        rs_copy(d).start()
    dup.wait_recv()
    ddown.wait_recv()
    for f in range(F // 2):
        light(f)
    total = pay[pl.ds(pl.multiple_of(me * rows, 8), rows), :]
    for d in range(1, nf):
        rs_copy(d).wait_recv()
        total = total + rs[d]
    own[...] = total
    for d in range(1, ns):
        sk_copy(d).start()
    for f in range(F // 2, F):
        light(f)
    for d in range(1, ns):
        sk_copy(d).wait_recv()
        total = total + sk[d]
    pay_out[pl.ds(pl.multiple_of(me * rows, 8), rows), :] = total
    for d in range(1, nf):
        ag_copy(d).start()
    for d in range(1, nf):
        ag_wait(d)

    up.wait_send()
    down.wait_send()
    dup.wait_send()
    ddown.wait_send()
    for d in range(1, nf):
        rs_copy(d).wait_send()
        ag_copy(d).wait_send()

        @pl.when(me >= d)
        def _():
            dec_copy(d).wait_send()
    for d in range(1, ns):
        sk_copy(d).wait_send()
    for d in range(1, chips):
        @pl.when(chip >= d)
        def _():
            cot_copy(d).wait_send()

        @pl.when(chip + d < chips)
        def _():
            fwd_copy(d).wait_send()

    @pl.when(core == 1)
    def _():
        sib_copy.wait_send()


def per_device(lightcone, cotangent, conv_weight, in_proj, out_proj, skip_gain, decay):
    F, C, R, W = lightcone.shape
    N = in_proj.shape[1]
    nf, ns = lax.axis_size("freq"), lax.axis_size("sky")
    scale = 1.0 / float(F * nf * R * ns * W) ** 0.5
    w4 = conv_weight.reshape(C, 3, 3, C)
    fw = w4.transpose(0, 2, 1, 3)
    bw = w4[:, ::-1].transpose(3, 2, 1, 0)

    def shifted(w, r):
        return jnp.pad(w, ((0, 0), (0, 0), (r, 1 - r), (0, 0))).reshape(C, 3 * 4 * C)

    a = jnp.concatenate([shifted(fw, 0), shifted(fw, 1)], axis=0)
    b = jnp.stack([shifted(bw, 0), shifted(bw, 1)], axis=1).reshape(2 * C, 3 * 4 * C)
    io = jnp.tile((in_proj * out_proj).reshape(1, C * N), (1, 4))
    skip4 = jnp.tile(skip_gain.reshape(1, C), (1, 4))
    rows = 128 // nf
    dma = pltpu.SemaphoreType.DMA
    vm = pl.BlockSpec(memory_space=pltpu.VMEM)
    dl, pay = pl.pallas_call(
        functools.partial(kernel, nf, ns),
        out_shape=(
            jax.ShapeDtypeStruct((F, C * R, W), BF),
            jax.ShapeDtypeStruct((128, 128), F32),
        ),
        in_specs=[vm] * 7,
        out_specs=(vm, vm),
        scratch_shapes=[
            pltpu.VMEM((F, 4 * C, W), BF),
            pltpu.VMEM((nf, F * C, R * W), BF),
            pltpu.VMEM((nf, F, C * N), F32),
            pltpu.VMEM((F * C, R * W), BF),
            pltpu.VMEM((F * C, R * W), F32),
            pltpu.VMEM((4 * F, 4 * C * N), F32),
            pltpu.VMEM((F, C * N), F32),
            pltpu.VMEM((4 * F, 128), F32),
            pltpu.VMEM((4 * F, 128), F32),
            pltpu.VMEM((F * C, F * C), BF),
            pltpu.VMEM((F, 4 * C, W), BF),
            pltpu.VMEM((8, 4 * C * N), F32),
            pltpu.VMEM((128, 128), F32),
            pltpu.VMEM((nf, rows, 128), F32),
            pltpu.VMEM((ns, rows, 128), F32),
            pltpu.VMEM((rows, 128), F32),
            dma((2,)), dma((2,)), dma((2,)), dma((2,)),
            dma((nf,)), dma((nf,)), dma((nf,)), dma((nf,)), dma((nf,)),
            dma((nf,)), dma((nf,)), dma((ns,)), dma((ns,)), dma((nf,)), dma((nf,)),
        ],
        compiler_params=pltpu.CompilerParams(
            collective_id=0, has_side_effects=True, vmem_limit_bytes=48 << 20),
    )(lightcone.reshape(F, C * R, W), cotangent.reshape(F, C * R, W), a, b, io, skip4, decay)
    grad = (pay[0:96, 0:96] * scale).reshape(3, C, 3, C).transpose(1, 2, 0, 3).reshape(C, 9 * C)
    t = (pay[96:100] * scale).reshape(C, N)
    d_skip = pay[100].reshape(4, C).sum(0) * scale
    return dl.reshape(F, C, R, W), grad, out_proj * t, in_proj * t, d_skip


def solution(mesh):
    return jax.shard_map(
        per_device,
        mesh=mesh,
        in_specs=(
            P(("replica", "freq"), None, "sky", None),
            P(("replica", "freq"), None, "sky", None),
            P(),
            P(),
            P(),
            P(),
            P("freq", None),
        ),
        out_specs=(
            P(("replica", "freq"), None, "sky", None),
            P("replica", None),
            P("replica", None),
            P("replica", None),
            P("replica"),
        ),
        check_vma=False,
    )
```

```python
import functools

import jax
import jax.numpy as jnp
from jax import lax
from jax.experimental import pallas as pl
from jax.experimental.pallas import tpu as pltpu
from jax.sharding import PartitionSpec as P

MESH = pl.DeviceIdType.MESH
BF = jnp.bfloat16
F32 = jnp.float32


def dot(a, b):
    return jnp.dot(a, b, preferred_element_type=F32)


def dot_nt(a, b):
    return lax.dot_general(a, b, (((1,), (1,)), ((), ())), preferred_element_type=F32)


def iota(shape, dim):
    return lax.broadcasted_iota(jnp.int32, shape, dim)


def kernel(nf, ns, x_ref, cot_ref, w_ref, in_ref, out_ref, skip_ref, dec_ref,
           dl_ref, pay_out,
           xr, cg, dg, inp, p4, cur, k4, m4, kb, dr, tacc, pay, rs, sk, own, aw, bw,
           halo_s, halo_r, dhalo_s, dhalo_r, dec_s, dec_r, cot_s, cot_r, fwd_s,
           rs_s, rs_r, sk_s, sk_r, ag_s, ag_r):
    F = x_ref.shape[0]
    me = lax.axis_index("freq")
    sky = lax.axis_index("sky")
    core = lax.rem(me, 2)
    chip = me // 2
    chips = nf // 2
    sibling = me + 1 - 2 * core
    nxt = lax.rem(sky + 1, ns)
    prv = lax.rem(sky + ns - 1, ns)
    rows = pay.shape[0] // nf

    barrier = pltpu.get_barrier_semaphore()
    for d in range(1, nf):
        pl.semaphore_signal(barrier, inc=1, device_id={"freq": lax.rem(me + d, nf)}, device_id_type=MESH)
    for d in range(1, ns):
        pl.semaphore_signal(barrier, inc=1, device_id={"sky": lax.rem(sky + d, ns)}, device_id_type=MESH)

    pr, pc = iota((64, 64), 0), iota((64, 64), 1)
    perm = (pc == 2 * lax.rem(pr, 32) + pr // 32).astype(F32).astype(BF)
    dg[me] = dec_ref[...]
    for f in range(F):
        c2 = dot(perm, cot_ref[f]).astype(BF)
        cg[me, 0, f * 32:(f + 1) * 32, :] = c2[0:32]
        cg[me, 1, f * 32:(f + 1) * 32, :] = c2[32:64]
    for f in range(F):
        xr[f, 32:96, :] = dot(perm, x_ref[f]).astype(BF)
    pl.semaphore_wait(barrier, nf + ns - 2)

    def remote(src, dst, s, r, **where):
        return pltpu.make_async_remote_copy(
            src_ref=src, dst_ref=dst, send_sem=s, recv_sem=r, device_id=dict(where), device_id_type=MESH)

    def dec_copy(d):
        return remote(dg.at[me], dg.at[me], dec_s.at[d], dec_r.at[me], freq=jnp.maximum(me - d, 0))

    def cot_copy(d, h):
        target = jnp.maximum(chip - d, 0) * 2 + core
        return remote(cg.at[me, h], cg.at[me, h], cot_s.at[d, h], cot_r.at[me, h], freq=target)

    def sib_copy(h):
        return remote(cg.at[me, h], cg.at[me, h], cot_s.at[0, h], cot_r.at[me, h], freq=sibling)

    def slot_copy(slot, h, s):
        return remote(cg.at[slot, h], cg.at[slot, h], s, cot_r.at[slot, h], freq=sibling)

    def fwd_copy(d, h):
        slot = jnp.minimum(chip + d, chips - 1) * 2 + core
        return slot_copy(slot, h, fwd_s.at[d, h])

    up = remote(xr.at[:, 64:96], xr.at[:, 0:32], halo_s.at[0], halo_r.at[0], sky=nxt)
    down = remote(xr.at[:, 32:64], xr.at[:, 96:128], halo_s.at[1], halo_r.at[1], sky=prv)
    for d in range(1, nf):
        @pl.when(me >= d)
        def _():
            dec_copy(d).start()
    for h in range(2):
        for d in range(1, chips):
            @pl.when(chip >= d)
            def _():
                cot_copy(d, h).start()

        @pl.when(core == 1)
        def _():
            sib_copy(h).start()
    up.start()
    down.start()

    sr, sc = iota((128, 256), 0), iota((128, 256), 1)
    shift = jnp.logical_or(lax.rem(sr + 1, 128) == sc, lax.rem(sr + 127, 128) == sc - 128)
    shift = shift.astype(F32).astype(BF)
    er = (iota((128, 2048), 1) // 16 == iota((128, 2048), 0)).astype(F32).astype(BF)
    et = (iota((2048, 128), 0) // 16 == iota((2048, 128), 1)).astype(F32).astype(BF)
    fi = iota((F, 512), 0)
    same = lax.rem(iota((32, 512), 1), 32) == iota((32, 512), 0)
    r64, l64 = iota((64, 128), 0), iota((64, 128), 1)
    diag = lax.rem(r64, 16) == 4 * (r64 // 16) + l64 // 32

    tacc[...] = jnp.zeros_like(tacc)
    cur[...] = jnp.zeros_like(cur)

    spread = (lax.rem(iota((32, 2048), 1) // 16, 32) == iota((32, 2048), 0)).astype(F32)
    io = jnp.dot(in_ref[...] * out_ref[...], spread, precision=lax.Precision.HIGHEST, preferred_element_type=F32)
    io = jnp.sum(jnp.where(lax.rem(iota((16, 2048), 1), 16) == iota((16, 2048), 0), io, 0.0), axis=0, keepdims=True)
    skip4 = jnp.concatenate([skip_ref[...]] * 4, axis=1)

    def factors(d, carry):
        q = me + d

        @pl.when(d > 0)
        def _():
            remote(dg.at[q], dg.at[q], dec_s.at[0], dec_r.at[q], freq=sibling).wait_recv()

        v = cur[...]
        for g in range(F):
            v = jnp.where(fi == g - F * d, 1.0, v * dg[q, g:g + 1, :])
            G, j = g // 4, g % 4
            p4[d, G * 16:(G + 1) * 16, j * 512:(j + 1) * 512] = v
        cur[...] = v
        k = dot((p4[d] * io).astype(BF), et)
        k4[...] = k + jnp.where(jnp.logical_and(diag, d == 0), skip4, 0.0)
        for f in range(F):
            for G in range(4):
                row = jnp.broadcast_to(k4[G * 16 + f:G * 16 + f + 1, :], (32, 128))
                kb[d, f * 32:(f + 1) * 32, G * 128:(G + 1) * 128] = jnp.where(same[:, 0:128], row, 0.0).astype(BF)
        return carry

    lax.fori_loop(0, nf - me, factors, 0)

    kk, ll = iota((288, 384), 0), iota((288, 384), 1)
    for r in range(2):
        tap = lax.rem(ll, 128) // 32 - r
        pick = jnp.logical_and(kk == (tap * 3 + ll // 128) * 32 + lax.rem(ll, 32),
                               jnp.logical_and(tap >= 0, tap <= 2))
        aw[r * 32:(r + 1) * 32, :] = dot(w_ref[...], pick.astype(F32).astype(BF)).astype(BF)
    mm, kk = iota((64, 288), 0), iota((64, 288), 1)
    for k in range(3):
        for row in range(4):
            tap = lax.rem(mm, 2) + 2 - row
            pick = jnp.logical_and(kk == (tap * 3 + k) * 32 + mm // 2,
                                   jnp.logical_and(tap >= 0, tap <= 2))
            at = k * 128 + row * 32
            bw[:, at:at + 32] = dot_nt(pick.astype(F32).astype(BF), w_ref[...])

    dup = remote(dr.at[:, 64:96], dr.at[:, 0:32], dhalo_s.at[1], dhalo_r.at[1], sky=nxt)
    ddown = remote(dr.at[:, 32:64], dr.at[:, 96:128], dhalo_s.at[0], dhalo_r.at[0], sky=prv)

    def mix(h):
        def step(d, total):
            q = me + d

            @pl.when(jnp.logical_and(d > 0, lax.rem(q, 2) == 0))
            def _():
                slot_copy(q + core, h, fwd_s.at[0, h]).wait_recv()
                slot_copy(q + core, h, fwd_s.at[q // 2 - chip, h]).start()

            @pl.when(jnp.logical_and(d > 0, lax.rem(q, 2) != core))
            def _():
                slot_copy(q, h, fwd_s.at[0, h]).wait_recv()

            return total + dot(kb[d], cg[q, h])

        total = lax.fori_loop(0, nf - me, step, jnp.zeros((F * 32, 128), F32)).astype(BF)
        for f in range(F):
            dr[f, 32 + 32 * h:64 + 32 * h, :] = total[f * 32:(f + 1) * 32]

    mix(0)
    ddown.start()
    up.wait_recv()
    down.wait_recv()
    for f in range(F):
        x = xr[f]
        rolled = dot(x, shift).astype(BF)
        full = jnp.concatenate([rolled[:, 0:128], x, rolled[:, 128:256]], axis=0)
        got = dot(aw[...], full).astype(BF)
        inp[f * 32:(f + 1) * 32, 0:128] = got[0:32]
        inp[f * 32:(f + 1) * 32, 128:256] = got[32:64]
    mix(1)
    dup.start()

    def block(d, carry):
        q = me + d
        gram = dot_nt(inp[...], jnp.concatenate([cg[q, 0], cg[q, 1]], axis=1))
        for f in range(F):
            row = jnp.sum(jnp.where(same, gram[f * 32:(f + 1) * 32, :], 0.0), axis=0, keepdims=True)
            for G in range(4):
                m4[G * 16 + f:G * 16 + f + 1, :] = row[:, G * 128:(G + 1) * 128]

        @pl.when(d == 0)
        def _():
            pay[96:128, :] = jnp.zeros((32, 128), F32)
            pay[100:101, :] = jnp.sum(jnp.where(diag, m4[...], 0.0), axis=0, keepdims=True)

        wide = dot(m4[...].astype(BF), er) * p4[d]
        tacc[...] += jnp.sum(wide.reshape(8, 8, 2048), axis=0)
        return carry

    lax.fori_loop(0, nf - me, block, 0)

    grad = jnp.zeros((192, 128), F32)
    for f in range(F):
        mid = dr[f, 32:96, :]
        rolled = dot(mid, shift).astype(BF)
        full = jnp.concatenate([rolled[:, 128:256], mid, rolled[:, 0:128]], axis=0)
        grad = grad + dot_nt(full, xr[f])
    for k in range(3):
        top = grad[k * 64:k * 64 + 32, 0:96]
        low = grad[k * 64 + 32:k * 64 + 64, 32:128]
        pay[k * 32:(k + 1) * 32, 0:96] = top + low
        pay[k * 32:(k + 1) * 32, 96:128] = jnp.zeros((32, 32), F32)
    t = jnp.sum(tacc[...], axis=0, keepdims=True)
    t = t[:, 0:512] + t[:, 512:1024] + t[:, 1024:1536] + t[:, 1536:2048]
    for k in range(4):
        pay[96 + k:97 + k, :] = t[:, k * 128:(k + 1) * 128]

    def part(ref, i):
        return ref.at[pl.ds(pl.multiple_of(i * rows, 8), rows)]

    def rs_copy(d):
        to = lax.rem(me + d, nf)
        return remote(part(pay, to), rs.at[d], rs_s.at[d], rs_r.at[d], freq=to)

    def sk_copy(d):
        return remote(own, sk.at[d], sk_s.at[d], sk_r.at[d], sky=lax.rem(sky + d, ns))

    def ag_copy(d):
        return remote(part(pay_out, me), part(pay_out, me), ag_s.at[d], ag_r.at[me],
                      freq=lax.rem(me + d, nf))

    def ag_wait(d):
        q = lax.rem(me + nf - d, nf)
        remote(part(pay_out, q), part(pay_out, q), ag_s.at[0], ag_r.at[q], freq=q).wait_recv()

    for d in range(1, nf):
        rs_copy(d).start()
    total = pay[pl.ds(pl.multiple_of(me * rows, 8), rows), :]
    for d in range(1, nf):
        rs_copy(d).wait_recv()
        total = total + rs[d]
    own[...] = total
    for d in range(1, ns):
        sk_copy(d).start()
    dup.wait_recv()
    ddown.wait_recv()
    b = bw[...].astype(BF)
    for f in range(F):
        x = dr[f]
        rolled = dot(x, shift).astype(BF)
        full = jnp.concatenate([rolled[:, 128:256], x, rolled[:, 0:128]], axis=0)
        dl_ref[f] = dot(b, full).astype(BF)
    for d in range(1, ns):
        sk_copy(d).wait_recv()
        total = total + sk[d]
    pay_out[pl.ds(pl.multiple_of(me * rows, 8), rows), :] = total
    for d in range(1, nf):
        ag_copy(d).start()
    for d in range(1, nf):
        ag_wait(d)

    up.wait_send()
    down.wait_send()
    dup.wait_send()
    ddown.wait_send()
    for d in range(1, nf):
        rs_copy(d).wait_send()
        ag_copy(d).wait_send()

        @pl.when(me >= d)
        def _():
            dec_copy(d).wait_send()
    for d in range(1, ns):
        sk_copy(d).wait_send()
    for h in range(2):
        for d in range(1, chips):
            @pl.when(chip >= d)
            def _():
                cot_copy(d, h).wait_send()

            @pl.when(chip + d < chips)
            def _():
                fwd_copy(d, h).wait_send()

        @pl.when(core == 1)
        def _():
            sib_copy(h).wait_send()


def finish(scale, dl_ref, pay_ref, in_ref, out_ref, dl_out, conv_out, din_out, dout_out, skip_out):
    dl_out[...] = dl_ref[...]
    for dr in range(3):
        for k in range(3):
            at = (dr * 3 + k) * 32
            conv_out[:, at:at + 32] = pay_ref[k * 32:(k + 1) * 32, dr * 32:(dr + 1) * 32] * scale
    t = jnp.concatenate([pay_ref[96 + k:97 + k, :] for k in range(4)], axis=1) * scale
    t = jnp.where(lax.rem(iota((16, 512), 1), 16) == iota((16, 512), 0), t, 0.0)
    join = (iota((512, 32), 0) // 16 == iota((512, 32), 1)).astype(F32)
    t = jnp.dot(t, join, precision=lax.Precision.HIGHEST, preferred_element_type=F32)
    din_out[...] = t * out_ref[...]
    dout_out[...] = t * in_ref[...]
    s = pay_ref[100:101, :] * scale
    skip_out[...] = s[:, 0:32] + s[:, 32:64] + s[:, 64:96] + s[:, 96:128]


def per_device(lightcone, cotangent, conv_weight, in_proj, out_proj, skip_gain, decay):
    F, C, R, W = lightcone.shape
    N = in_proj.shape[1]
    nf, ns = lax.axis_size("freq"), lax.axis_size("sky")
    scale = 1.0 / float(F * nf * R * ns * W) ** 0.5
    rows = 128 // nf
    dma = pltpu.SemaphoreType.DMA
    vm = pl.BlockSpec(memory_space=pltpu.VMEM)
    dl, pay = pl.pallas_call(
        functools.partial(kernel, nf, ns),
        out_shape=(
            jax.ShapeDtypeStruct((F, C * R, W), BF),
            jax.ShapeDtypeStruct((128, 128), F32),
        ),
        in_specs=[vm] * 7,
        out_specs=(vm, vm),
        scratch_shapes=[
            pltpu.VMEM((F, 4 * C, W), BF),
            pltpu.VMEM((nf, R, F * C, W), BF),
            pltpu.VMEM((nf, F, C * N), F32),
            pltpu.VMEM((F * C, R * W), BF),
            pltpu.VMEM((nf, 4 * F, 4 * C * N), F32),
            pltpu.VMEM((F, C * N), F32),
            pltpu.VMEM((4 * F, 128), F32),
            pltpu.VMEM((4 * F, 128), F32),
            pltpu.VMEM((nf, F * C, F * C), BF),
            pltpu.VMEM((F, 4 * C, W), BF),
            pltpu.VMEM((8, 4 * C * N), F32),
            pltpu.VMEM((128, 128), F32),
            pltpu.VMEM((nf, rows, 128), F32),
            pltpu.VMEM((ns, rows, 128), F32),
            pltpu.VMEM((rows, 128), F32),
            pltpu.VMEM((2 * C, 12 * C), BF),
            pltpu.VMEM((2 * C, 12 * C), F32),
            dma((2,)), dma((2,)), dma((2,)), dma((2,)),
            dma((nf,)), dma((nf,)), dma((nf, 2)), dma((nf, 2)), dma((nf, 2)),
            dma((nf,)), dma((nf,)), dma((ns,)), dma((ns,)), dma((nf,)), dma((nf,)),
        ],
        compiler_params=pltpu.CompilerParams(
            collective_id=0, has_side_effects=True, vmem_limit_bytes=48 << 20),
    )(lightcone.reshape(F, C * R, W), cotangent.reshape(F, C * R, W), conv_weight,
      in_proj.T, out_proj.T, skip_gain.reshape(1, C), decay)
    dl, grad, din, dout, d_skip = pl.pallas_call(
        functools.partial(finish, scale),
        out_shape=(
            jax.ShapeDtypeStruct((F, C * R, W), BF),
            jax.ShapeDtypeStruct((C, 9 * C), F32),
            jax.ShapeDtypeStruct((N, C), F32),
            jax.ShapeDtypeStruct((N, C), F32),
            jax.ShapeDtypeStruct((1, C), F32),
        ),
        in_specs=[vm] * 4,
        out_specs=(vm,) * 5,
        compiler_params=pltpu.CompilerParams(vmem_limit_bytes=4 << 20),
    )(dl, pay, in_proj.T, out_proj.T)
    return dl.reshape(F, C, R, W), grad, din.T, dout.T, d_skip.reshape(C)


def solution(mesh):
    return jax.shard_map(
        per_device,
        mesh=mesh,
        in_specs=(
            P(("replica", "freq"), None, "sky", None),
            P(("replica", "freq"), None, "sky", None),
            P(),
            P(),
            P(),
            P(),
            P("freq", None),
        ),
        out_specs=(
            P(("replica", "freq"), None, "sky", None),
            P("replica", None),
            P("replica", None),
            P("replica", None),
            P("replica"),
        ),
        check_vma=False,
    )
```

```python
import functools

import jax
import jax.numpy as jnp
from jax import lax
from jax.experimental import pallas as pl
from jax.experimental.pallas import tpu as pltpu
from jax.sharding import PartitionSpec as P

MESH = pl.DeviceIdType.MESH
BF = jnp.bfloat16
F32 = jnp.float32


def dot(a, b):
    return jnp.dot(a, b, preferred_element_type=F32)


def dot_nt(a, b):
    return lax.dot_general(a, b, (((1,), (1,)), ((), ())), preferred_element_type=F32)


def iota(shape, dim):
    return lax.broadcasted_iota(jnp.int32, shape, dim)


def kernel(nf, ns, x_hbm, cot_hbm, w_hbm, in_hbm, out_hbm, skip_hbm, dec_hbm,
           dl_ref, pay_out,
           xr, cg, dg, inp, p4, cur, k4, m4, kb, dr, tacc, pay, rs, sk, own, aw, bw,
           halo_s, halo_r, dhalo_s, dhalo_r, dec_s, dec_r, cot_s, cot_r, fwd_s,
           rs_s, rs_r, sk_s, sk_r, ag_s, ag_r,
           x_ref, cot_ref, w_ref, in_ref, out_ref, skip_ref, load):
    F = x_ref.shape[0]
    me = lax.axis_index("freq")
    sky = lax.axis_index("sky")
    core = lax.rem(me, 2)
    chip = me // 2
    chips = nf // 2
    sibling = me + 1 - 2 * core
    nxt = lax.rem(sky + 1, ns)
    prv = lax.rem(sky + ns - 1, ns)
    rows = pay.shape[0] // nf

    loads = [
        pltpu.make_async_copy(src, dst, load.at[i])
        for i, (src, dst) in enumerate((
            (cot_hbm, cot_ref), (dec_hbm, dg.at[me]), (x_hbm, x_ref), (w_hbm, w_ref),
            (in_hbm, in_ref), (out_hbm, out_ref), (skip_hbm, skip_ref)))
    ]
    for one in loads:
        one.start()
    barrier = pltpu.get_barrier_semaphore()
    for d in range(1, nf):
        pl.semaphore_signal(barrier, inc=1, device_id={"freq": lax.rem(me + d, nf)}, device_id_type=MESH)
    for d in range(1, ns):
        pl.semaphore_signal(barrier, inc=1, device_id={"sky": lax.rem(sky + d, ns)}, device_id_type=MESH)

    pr, pc = iota((64, 64), 0), iota((64, 64), 1)
    perm = (pc == 2 * lax.rem(pr, 32) + pr // 32).astype(F32).astype(BF)
    loads[0].wait()
    for f in range(F):
        c2 = dot(perm, cot_ref[f]).astype(BF)
        cg[me, 0, f * 32:(f + 1) * 32, :] = c2[0:32]
        cg[me, 1, f * 32:(f + 1) * 32, :] = c2[32:64]
    loads[2].wait()
    for f in range(F):
        xr[f, 32:96, :] = dot(perm, x_ref[f]).astype(BF)
    for i in (1, 3, 4, 5, 6):
        loads[i].wait()
    pl.semaphore_wait(barrier, nf + ns - 2)

    def remote(src, dst, s, r, **where):
        return pltpu.make_async_remote_copy(
            src_ref=src, dst_ref=dst, send_sem=s, recv_sem=r, device_id=dict(where), device_id_type=MESH)

    def dec_copy(d):
        return remote(dg.at[me], dg.at[me], dec_s.at[d], dec_r.at[me], freq=jnp.maximum(me - d, 0))

    def cot_copy(d, h):
        target = jnp.maximum(chip - d, 0) * 2 + core
        return remote(cg.at[me, h], cg.at[me, h], cot_s.at[d, h], cot_r.at[me, h], freq=target)

    def sib_copy(h):
        return remote(cg.at[me, h], cg.at[me, h], cot_s.at[0, h], cot_r.at[me, h], freq=sibling)

    def slot_copy(slot, h, s):
        return remote(cg.at[slot, h], cg.at[slot, h], s, cot_r.at[slot, h], freq=sibling)

    def fwd_copy(d, h):
        slot = jnp.minimum(chip + d, chips - 1) * 2 + core
        return slot_copy(slot, h, fwd_s.at[d, h])

    up = remote(xr.at[:, 64:96], xr.at[:, 0:32], halo_s.at[0], halo_r.at[0], sky=nxt)
    down = remote(xr.at[:, 32:64], xr.at[:, 96:128], halo_s.at[1], halo_r.at[1], sky=prv)
    for d in range(1, nf):
        @pl.when(me >= d)
        def _():
            dec_copy(d).start()
    for h in range(2):
        for d in range(1, chips):
            @pl.when(chip >= d)
            def _():
                cot_copy(d, h).start()

        @pl.when(core == 1)
        def _():
            sib_copy(h).start()
    up.start()
    down.start()

    sr, sc = iota((128, 256), 0), iota((128, 256), 1)
    shift = jnp.logical_or(lax.rem(sr + 1, 128) == sc, lax.rem(sr + 127, 128) == sc - 128)
    shift = shift.astype(F32).astype(BF)
    er = (iota((128, 2048), 1) // 16 == iota((128, 2048), 0)).astype(F32).astype(BF)
    et = (iota((2048, 128), 0) // 16 == iota((2048, 128), 1)).astype(F32).astype(BF)
    fi = iota((F, 512), 0)
    same = lax.rem(iota((32, 512), 1), 32) == iota((32, 512), 0)
    r64, l64 = iota((64, 128), 0), iota((64, 128), 1)
    diag = lax.rem(r64, 16) == 4 * (r64 // 16) + l64 // 32

    tacc[...] = jnp.zeros_like(tacc)
    cur[...] = jnp.zeros_like(cur)

    spread = (lax.rem(iota((32, 2048), 1) // 16, 32) == iota((32, 2048), 0)).astype(F32)
    io = jnp.dot(in_ref[...] * out_ref[...], spread, precision=lax.Precision.HIGHEST, preferred_element_type=F32)
    io = jnp.sum(jnp.where(lax.rem(iota((16, 2048), 1), 16) == iota((16, 2048), 0), io, 0.0), axis=0, keepdims=True)
    skip4 = jnp.concatenate([skip_ref[...]] * 4, axis=1)

    def factors(d, carry):
        q = me + d

        @pl.when(d > 0)
        def _():
            remote(dg.at[q], dg.at[q], dec_s.at[0], dec_r.at[q], freq=sibling).wait_recv()

        v = cur[...]
        for g in range(F):
            v = jnp.where(fi == g - F * d, 1.0, v * dg[q, g:g + 1, :])
            G, j = g // 4, g % 4
            p4[d, G * 16:(G + 1) * 16, j * 512:(j + 1) * 512] = v
        cur[...] = v
        k = dot((p4[d] * io).astype(BF), et)
        k4[...] = k + jnp.where(jnp.logical_and(diag, d == 0), skip4, 0.0)
        for f in range(F):
            for G in range(4):
                row = jnp.broadcast_to(k4[G * 16 + f:G * 16 + f + 1, :], (32, 128))
                kb[d, f * 32:(f + 1) * 32, G * 128:(G + 1) * 128] = jnp.where(same[:, 0:128], row, 0.0).astype(BF)
        return carry

    lax.fori_loop(0, nf - me, factors, 0)

    kk, ll = iota((288, 384), 0), iota((288, 384), 1)
    for r in range(2):
        tap = lax.rem(ll, 128) // 32 - r
        pick = jnp.logical_and(kk == (tap * 3 + ll // 128) * 32 + lax.rem(ll, 32),
                               jnp.logical_and(tap >= 0, tap <= 2))
        aw[r * 32:(r + 1) * 32, :] = dot(w_ref[...], pick.astype(F32).astype(BF)).astype(BF)
    mm, kk = iota((64, 288), 0), iota((64, 288), 1)
    for k in range(3):
        for row in range(4):
            tap = lax.rem(mm, 2) + 2 - row
            pick = jnp.logical_and(kk == (tap * 3 + k) * 32 + mm // 2,
                                   jnp.logical_and(tap >= 0, tap <= 2))
            at = k * 128 + row * 32
            bw[:, at:at + 32] = dot_nt(pick.astype(F32).astype(BF), w_ref[...])

    dup = remote(dr.at[:, 64:96], dr.at[:, 0:32], dhalo_s.at[1], dhalo_r.at[1], sky=nxt)
    ddown = remote(dr.at[:, 32:64], dr.at[:, 96:128], dhalo_s.at[0], dhalo_r.at[0], sky=prv)

    def mix(h):
        def step(d, total):
            q = me + d

            @pl.when(jnp.logical_and(d > 0, lax.rem(q, 2) == 0))
            def _():
                slot_copy(q + core, h, fwd_s.at[0, h]).wait_recv()
                slot_copy(q + core, h, fwd_s.at[q // 2 - chip, h]).start()

            @pl.when(jnp.logical_and(d > 0, lax.rem(q, 2) != core))
            def _():
                slot_copy(q, h, fwd_s.at[0, h]).wait_recv()

            return total + dot(kb[d], cg[q, h])

        total = lax.fori_loop(0, nf - me, step, jnp.zeros((F * 32, 128), F32)).astype(BF)
        for f in range(F):
            dr[f, 32 + 32 * h:64 + 32 * h, :] = total[f * 32:(f + 1) * 32]

    mix(0)
    ddown.start()
    up.wait_recv()
    down.wait_recv()
    for f in range(F):
        x = xr[f]
        rolled = dot(x, shift).astype(BF)
        full = jnp.concatenate([rolled[:, 0:128], x, rolled[:, 128:256]], axis=0)
        got = dot(aw[...], full).astype(BF)
        inp[f * 32:(f + 1) * 32, 0:128] = got[0:32]
        inp[f * 32:(f + 1) * 32, 128:256] = got[32:64]
    mix(1)
    dup.start()

    def block(d, carry):
        q = me + d
        gram = dot_nt(inp[...], jnp.concatenate([cg[q, 0], cg[q, 1]], axis=1))
        for f in range(F):
            row = jnp.sum(jnp.where(same, gram[f * 32:(f + 1) * 32, :], 0.0), axis=0, keepdims=True)
            for G in range(4):
                m4[G * 16 + f:G * 16 + f + 1, :] = row[:, G * 128:(G + 1) * 128]

        @pl.when(d == 0)
        def _():
            pay[96:128, :] = jnp.zeros((32, 128), F32)
            pay[100:101, :] = jnp.sum(jnp.where(diag, m4[...], 0.0), axis=0, keepdims=True)

        wide = dot(m4[...].astype(BF), er) * p4[d]
        tacc[...] += jnp.sum(wide.reshape(8, 8, 2048), axis=0)
        return carry

    lax.fori_loop(0, nf - me, block, 0)

    grad = jnp.zeros((192, 128), F32)
    for f in range(F):
        mid = dr[f, 32:96, :]
        rolled = dot(mid, shift).astype(BF)
        full = jnp.concatenate([rolled[:, 128:256], mid, rolled[:, 0:128]], axis=0)
        grad = grad + dot_nt(full, xr[f])
    for k in range(3):
        top = grad[k * 64:k * 64 + 32, 0:96]
        low = grad[k * 64 + 32:k * 64 + 64, 32:128]
        pay[k * 32:(k + 1) * 32, 0:96] = top + low
        pay[k * 32:(k + 1) * 32, 96:128] = jnp.zeros((32, 32), F32)
    t = jnp.sum(tacc[...], axis=0, keepdims=True)
    t = t[:, 0:512] + t[:, 512:1024] + t[:, 1024:1536] + t[:, 1536:2048]
    for k in range(4):
        pay[96 + k:97 + k, :] = t[:, k * 128:(k + 1) * 128]

    def part(ref, i):
        return ref.at[pl.ds(pl.multiple_of(i * rows, 8), rows)]

    def rs_copy(d):
        to = lax.rem(me + d, nf)
        return remote(part(pay, to), rs.at[d], rs_s.at[d], rs_r.at[d], freq=to)

    def sk_copy(d):
        return remote(own, sk.at[d], sk_s.at[d], sk_r.at[d], sky=lax.rem(sky + d, ns))

    def ag_copy(d):
        return remote(part(pay_out, me), part(pay_out, me), ag_s.at[d], ag_r.at[me],
                      freq=lax.rem(me + d, nf))

    def ag_wait(d):
        q = lax.rem(me + nf - d, nf)
        remote(part(pay_out, q), part(pay_out, q), ag_s.at[0], ag_r.at[q], freq=q).wait_recv()

    for d in range(1, nf):
        rs_copy(d).start()
    total = pay[pl.ds(pl.multiple_of(me * rows, 8), rows), :]
    for d in range(1, nf):
        rs_copy(d).wait_recv()
        total = total + rs[d]
    own[...] = total
    for d in range(1, ns):
        sk_copy(d).start()
    dup.wait_recv()
    ddown.wait_recv()
    b = bw[...].astype(BF)
    for f in range(F):
        x = dr[f]
        rolled = dot(x, shift).astype(BF)
        full = jnp.concatenate([rolled[:, 128:256], x, rolled[:, 0:128]], axis=0)
        dl_ref[f] = dot(b, full).astype(BF)
    for d in range(1, ns):
        sk_copy(d).wait_recv()
        total = total + sk[d]
    pay_out[pl.ds(pl.multiple_of(me * rows, 8), rows), :] = total
    for d in range(1, nf):
        ag_copy(d).start()
    for d in range(1, nf):
        ag_wait(d)

    up.wait_send()
    down.wait_send()
    dup.wait_send()
    ddown.wait_send()
    for d in range(1, nf):
        rs_copy(d).wait_send()
        ag_copy(d).wait_send()

        @pl.when(me >= d)
        def _():
            dec_copy(d).wait_send()
    for d in range(1, ns):
        sk_copy(d).wait_send()
    for h in range(2):
        for d in range(1, chips):
            @pl.when(chip >= d)
            def _():
                cot_copy(d, h).wait_send()

            @pl.when(chip + d < chips)
            def _():
                fwd_copy(d, h).wait_send()

        @pl.when(core == 1)
        def _():
            sib_copy(h).wait_send()


def finish(scale, dl_ref, pay_ref, in_ref, out_ref, dl_out, conv_out, din_out, dout_out, skip_out):
    dl_out[...] = dl_ref[...]
    for dr in range(3):
        for k in range(3):
            at = (dr * 3 + k) * 32
            conv_out[:, at:at + 32] = pay_ref[k * 32:(k + 1) * 32, dr * 32:(dr + 1) * 32] * scale
    t = jnp.concatenate([pay_ref[96 + k:97 + k, :] for k in range(4)], axis=1) * scale
    t = jnp.where(lax.rem(iota((16, 512), 1), 16) == iota((16, 512), 0), t, 0.0)
    join = (iota((512, 32), 0) // 16 == iota((512, 32), 1)).astype(F32)
    t = jnp.dot(t, join, precision=lax.Precision.HIGHEST, preferred_element_type=F32)
    din_out[...] = t * out_ref[...]
    dout_out[...] = t * in_ref[...]
    s = pay_ref[100:101, :] * scale
    skip_out[...] = s[:, 0:32] + s[:, 32:64] + s[:, 64:96] + s[:, 96:128]


def per_device(lightcone, cotangent, conv_weight, in_proj, out_proj, skip_gain, decay):
    F, C, R, W = lightcone.shape
    N = in_proj.shape[1]
    nf, ns = lax.axis_size("freq"), lax.axis_size("sky")
    scale = 1.0 / float(F * nf * R * ns * W) ** 0.5
    rows = 128 // nf
    dma = pltpu.SemaphoreType.DMA
    vm = pl.BlockSpec(memory_space=pltpu.VMEM)
    dl, pay = pl.pallas_call(
        functools.partial(kernel, nf, ns),
        out_shape=(
            jax.ShapeDtypeStruct((F, C * R, W), BF),
            jax.ShapeDtypeStruct((128, 128), F32),
        ),
        in_specs=[pl.BlockSpec(memory_space=pltpu.MemorySpace.HBM)] * 7,
        out_specs=(vm, vm),
        scratch_shapes=[
            pltpu.VMEM((F, 4 * C, W), BF),
            pltpu.VMEM((nf, R, F * C, W), BF),
            pltpu.VMEM((nf, F, C * N), F32),
            pltpu.VMEM((F * C, R * W), BF),
            pltpu.VMEM((nf, 4 * F, 4 * C * N), F32),
            pltpu.VMEM((F, C * N), F32),
            pltpu.VMEM((4 * F, 128), F32),
            pltpu.VMEM((4 * F, 128), F32),
            pltpu.VMEM((nf, F * C, F * C), BF),
            pltpu.VMEM((F, 4 * C, W), BF),
            pltpu.VMEM((8, 4 * C * N), F32),
            pltpu.VMEM((128, 128), F32),
            pltpu.VMEM((nf, rows, 128), F32),
            pltpu.VMEM((ns, rows, 128), F32),
            pltpu.VMEM((rows, 128), F32),
            pltpu.VMEM((2 * C, 12 * C), BF),
            pltpu.VMEM((2 * C, 12 * C), F32),
            dma((2,)), dma((2,)), dma((2,)), dma((2,)),
            dma((nf,)), dma((nf,)), dma((nf, 2)), dma((nf, 2)), dma((nf, 2)),
            dma((nf,)), dma((nf,)), dma((ns,)), dma((ns,)), dma((nf,)), dma((nf,)),
            pltpu.VMEM((F, C * R, W), BF),
            pltpu.VMEM((F, C * R, W), BF),
            pltpu.VMEM((C, 9 * C), BF),
            pltpu.VMEM((N, C), F32),
            pltpu.VMEM((N, C), F32),
            pltpu.VMEM((1, C), F32),
            dma((7,)),
        ],
        compiler_params=pltpu.CompilerParams(
            collective_id=0, has_side_effects=True, vmem_limit_bytes=63 << 20),
    )(lightcone.reshape(F, C * R, W), cotangent.reshape(F, C * R, W), conv_weight,
      in_proj.T, out_proj.T, skip_gain.reshape(1, C), decay)
    dl, grad, din, dout, d_skip = pl.pallas_call(
        functools.partial(finish, scale),
        out_shape=(
            jax.ShapeDtypeStruct((F, C * R, W), BF),
            jax.ShapeDtypeStruct((C, 9 * C), F32),
            jax.ShapeDtypeStruct((N, C), F32),
            jax.ShapeDtypeStruct((N, C), F32),
            jax.ShapeDtypeStruct((1, C), F32),
        ),
        in_specs=[vm] * 4,
        out_specs=(vm,) * 5,
        compiler_params=pltpu.CompilerParams(vmem_limit_bytes=63 << 20),
    )(dl, pay, in_proj.T, out_proj.T)
    return dl.reshape(F, C, R, W), grad, din.T, dout.T, d_skip.reshape(C)


def solution(mesh):
    return jax.shard_map(
        per_device,
        mesh=mesh,
        in_specs=(
            P(("replica", "freq"), None, "sky", None),
            P(("replica", "freq"), None, "sky", None),
            P(),
            P(),
            P(),
            P(),
            P("freq", None),
        ),
        out_specs=(
            P(("replica", "freq"), None, "sky", None),
            P("replica", None),
            P("replica", None),
            P("replica", None),
            P("replica"),
        ),
        check_vma=False,
    )
```

```python
import functools

import jax
import jax.numpy as jnp
from jax import lax
from jax.experimental import pallas as pl
from jax.experimental.pallas import tpu as pltpu
from jax.sharding import PartitionSpec as P

MESH = pl.DeviceIdType.MESH
BF = jnp.bfloat16
F32 = jnp.float32


def dot(a, b):
    return jnp.dot(a, b, preferred_element_type=F32)


def dot_nt(a, b):
    return lax.dot_general(a, b, (((1,), (1,)), ((), ())), preferred_element_type=F32)


def iota(shape, dim):
    return lax.broadcasted_iota(jnp.int32, shape, dim)


def kernel(nf, ns, x_hbm, cot_hbm, w_hbm, in_hbm, out_hbm, skip_hbm, dec_hbm,
           dl_ref, pay_out,
           xr, cg, dg, inp, p4, cur, k4, m4, kb, dr, tacc, pay, rs, sk, own, aw, bw,
           halo_s, halo_r, dhalo_s, dhalo_r, dec_s, dec_r, cot_s, cot_r, fwd_s,
           rs_s, rs_r, sk_s, sk_r, ag_s, ag_r,
           x_ref, cot_ref, w_ref, in_ref, out_ref, skip_ref, load):
    F = x_ref.shape[0]
    me = lax.axis_index("freq")
    sky = lax.axis_index("sky")
    core = lax.rem(me, 2)
    chip = me // 2
    chips = nf // 2
    sibling = me + 1 - 2 * core
    nxt = lax.rem(sky + 1, ns)
    prv = lax.rem(sky + ns - 1, ns)
    rows = pay.shape[0] // nf

    loads = [
        pltpu.make_async_copy(src, dst, load.at[i])
        for i, (src, dst) in enumerate((
            (cot_hbm, cot_ref), (dec_hbm, dg.at[me]), (x_hbm, x_ref), (w_hbm, w_ref),
            (in_hbm, in_ref), (out_hbm, out_ref), (skip_hbm, skip_ref)))
    ]
    for one in loads:
        one.start()
    barrier = pltpu.get_barrier_semaphore()
    for d in range(1, nf):
        pl.semaphore_signal(barrier, inc=1, device_id={"freq": lax.rem(me + d, nf)}, device_id_type=MESH)
    for d in range(1, ns):
        pl.semaphore_signal(barrier, inc=1, device_id={"sky": lax.rem(sky + d, ns)}, device_id_type=MESH)

    pr, pc = iota((64, 64), 0), iota((64, 64), 1)
    perm = (pc == 2 * lax.rem(pr, 32) + pr // 32).astype(F32).astype(BF)
    loads[0].wait()
    for f in range(F):
        c2 = dot(perm, cot_ref[f]).astype(BF)
        cg[me, 0, f * 32:(f + 1) * 32, :] = c2[0:32]
        cg[me, 1, f * 32:(f + 1) * 32, :] = c2[32:64]
    loads[2].wait()
    for f in range(F):
        xr[f, 32:96, :] = dot(perm, x_ref[f]).astype(BF)
    for i in (1, 3, 4, 5, 6):
        loads[i].wait()
    pl.semaphore_wait(barrier, nf + ns - 2)

    def remote(src, dst, s, r, **where):
        return pltpu.make_async_remote_copy(
            src_ref=src, dst_ref=dst, send_sem=s, recv_sem=r, device_id=dict(where), device_id_type=MESH)

    def dec_copy(d):
        return remote(dg.at[me], dg.at[me], dec_s.at[d], dec_r.at[me], freq=jnp.maximum(me - d, 0))

    def cot_copy(d, h):
        target = jnp.maximum(chip - d, 0) * 2 + core
        return remote(cg.at[me, h], cg.at[me, h], cot_s.at[d, h], cot_r.at[me, h], freq=target)

    def sib_copy(h):
        return remote(cg.at[me, h], cg.at[me, h], cot_s.at[0, h], cot_r.at[me, h], freq=sibling)

    def slot_copy(slot, h, s):
        return remote(cg.at[slot, h], cg.at[slot, h], s, cot_r.at[slot, h], freq=sibling)

    def fwd_copy(d, h):
        slot = jnp.minimum(chip + d, chips - 1) * 2 + core
        return slot_copy(slot, h, fwd_s.at[d, h])

    up = remote(xr.at[:, 64:96], xr.at[:, 0:32], halo_s.at[0], halo_r.at[0], sky=nxt)
    down = remote(xr.at[:, 32:64], xr.at[:, 96:128], halo_s.at[1], halo_r.at[1], sky=prv)
    for d in range(1, nf):
        @pl.when(me >= d)
        def _():
            dec_copy(d).start()
    for h in range(2):
        for d in range(1, chips):
            @pl.when(chip >= d)
            def _():
                cot_copy(d, h).start()

        @pl.when(core == 1)
        def _():
            sib_copy(h).start()
    up.start()
    down.start()

    sr, sc = iota((128, 256), 0), iota((128, 256), 1)
    shift = jnp.logical_or(lax.rem(sr + 1, 128) == sc, lax.rem(sr + 127, 128) == sc - 128)
    shift = shift.astype(F32).astype(BF)
    er = (iota((128, 2048), 1) // 16 == iota((128, 2048), 0)).astype(F32).astype(BF)
    et = (iota((2048, 128), 0) // 16 == iota((2048, 128), 1)).astype(F32).astype(BF)
    fi = iota((F, 512), 0)
    same = lax.rem(iota((32, 512), 1), 32) == iota((32, 512), 0)
    r64, l64 = iota((64, 128), 0), iota((64, 128), 1)
    diag = lax.rem(r64, 16) == 4 * (r64 // 16) + l64 // 32

    tacc[...] = jnp.zeros_like(tacc)
    cur[...] = jnp.zeros_like(cur)

    spread = (lax.rem(iota((32, 2048), 1) // 16, 32) == iota((32, 2048), 0)).astype(F32)
    io = jnp.dot(in_ref[...] * out_ref[...], spread, precision=lax.Precision.HIGHEST, preferred_element_type=F32)
    io = jnp.sum(jnp.where(lax.rem(iota((16, 2048), 1), 16) == iota((16, 2048), 0), io, 0.0), axis=0, keepdims=True)
    skip4 = jnp.concatenate([skip_ref[...]] * 4, axis=1)

    def factors(d, carry):
        q = me + d

        @pl.when(d > 0)
        def _():
            remote(dg.at[q], dg.at[q], dec_s.at[0], dec_r.at[q], freq=sibling).wait_recv()

        v = cur[...]
        for g in range(F):
            v = jnp.where(fi == g - F * d, 1.0, v * dg[q, g:g + 1, :])
            G, j = g // 4, g % 4
            p4[d, G * 16:(G + 1) * 16, j * 512:(j + 1) * 512] = v
        cur[...] = v
        k = dot((p4[d] * io).astype(BF), et)
        k4[...] = k + jnp.where(jnp.logical_and(diag, d == 0), skip4, 0.0)
        for f in range(F):
            for G in range(4):
                row = jnp.broadcast_to(k4[G * 16 + f:G * 16 + f + 1, :], (32, 128))
                kb[d, f * 32:(f + 1) * 32, G * 128:(G + 1) * 128] = jnp.where(same[:, 0:128], row, 0.0).astype(BF)
        return carry

    lax.fori_loop(0, nf - me, factors, 0)

    kk, ll = iota((288, 384), 0), iota((288, 384), 1)
    for r in range(2):
        tap = lax.rem(ll, 128) // 32 - r
        pick = jnp.logical_and(kk == (tap * 3 + ll // 128) * 32 + lax.rem(ll, 32),
                               jnp.logical_and(tap >= 0, tap <= 2))
        aw[r * 32:(r + 1) * 32, :] = dot(w_ref[...], pick.astype(F32).astype(BF)).astype(BF)
    mm, kk = iota((64, 288), 0), iota((64, 288), 1)
    for k in range(3):
        for row in range(4):
            tap = lax.rem(mm, 2) + 2 - row
            pick = jnp.logical_and(kk == (tap * 3 + k) * 32 + mm // 2,
                                   jnp.logical_and(tap >= 0, tap <= 2))
            at = k * 128 + row * 32
            bw[:, at:at + 32] = dot_nt(pick.astype(F32).astype(BF), w_ref[...])

    dup = remote(dr.at[:, 64:96], dr.at[:, 0:32], dhalo_s.at[1], dhalo_r.at[1], sky=nxt)
    ddown = remote(dr.at[:, 32:64], dr.at[:, 96:128], dhalo_s.at[0], dhalo_r.at[0], sky=prv)

    def mix(h):
        def step(d, total):
            q = me + d

            @pl.when(jnp.logical_and(d > 0, lax.rem(q, 2) == 0))
            def _():
                slot_copy(q + core, h, fwd_s.at[0, h]).wait_recv()
                slot_copy(q + core, h, fwd_s.at[q // 2 - chip, h]).start()

            @pl.when(jnp.logical_and(d > 0, lax.rem(q, 2) != core))
            def _():
                slot_copy(q, h, fwd_s.at[0, h]).wait_recv()

            return total + dot(kb[d], cg[q, h])

        total = lax.fori_loop(0, nf - me, step, jnp.zeros((F * 32, 128), F32)).astype(BF)
        for f in range(F):
            dr[f, 32 + 32 * h:64 + 32 * h, :] = total[f * 32:(f + 1) * 32]

    mix(0)
    ddown.start()
    up.wait_recv()
    down.wait_recv()
    for f in range(F):
        x = xr[f]
        rolled = dot(x, shift).astype(BF)
        full = jnp.concatenate([rolled[:, 0:128], x, rolled[:, 128:256]], axis=0)
        got = dot(aw[...], full).astype(BF)
        inp[f * 32:(f + 1) * 32, 0:128] = got[0:32]
        inp[f * 32:(f + 1) * 32, 128:256] = got[32:64]
    mix(1)
    dup.start()

    def block(d, carry):
        q = me + d
        gram = dot_nt(inp[...], jnp.concatenate([cg[q, 0], cg[q, 1]], axis=1))
        for f in range(F):
            row = jnp.sum(jnp.where(same, gram[f * 32:(f + 1) * 32, :], 0.0), axis=0, keepdims=True)
            for G in range(4):
                m4[G * 16 + f:G * 16 + f + 1, :] = row[:, G * 128:(G + 1) * 128]

        @pl.when(d == 0)
        def _():
            pay[96:128, :] = jnp.zeros((32, 128), F32)
            pay[100:101, :] = jnp.sum(jnp.where(diag, m4[...], 0.0), axis=0, keepdims=True)

        wide = dot(m4[...].astype(BF), er) * p4[d]
        tacc[...] += jnp.sum(wide.reshape(8, 8, 2048), axis=0)
        return carry

    lax.fori_loop(0, nf - me, block, 0)

    grad = jnp.zeros((192, 128), F32)
    for f in range(F):
        mid = dr[f, 32:96, :]
        rolled = dot(mid, shift).astype(BF)
        full = jnp.concatenate([rolled[:, 128:256], mid, rolled[:, 0:128]], axis=0)
        grad = grad + dot_nt(full, xr[f])
    for k in range(3):
        top = grad[k * 64:k * 64 + 32, 0:96]
        low = grad[k * 64 + 32:k * 64 + 64, 32:128]
        pay[k * 32:(k + 1) * 32, 0:96] = top + low
        pay[k * 32:(k + 1) * 32, 96:128] = jnp.zeros((32, 32), F32)
    t = jnp.sum(tacc[...], axis=0, keepdims=True)
    t = t[:, 0:512] + t[:, 512:1024] + t[:, 1024:1536] + t[:, 1536:2048]
    for k in range(4):
        pay[96 + k:97 + k, :] = t[:, k * 128:(k + 1) * 128]

    def part(ref, i):
        return ref.at[pl.ds(pl.multiple_of(i * rows, 8), rows)]

    def rs_copy(d):
        to = lax.rem(me + d, nf)
        return remote(part(pay, to), rs.at[d], rs_s.at[d], rs_r.at[d], freq=to)

    def sk_copy(d):
        return remote(own, sk.at[d], sk_s.at[d], sk_r.at[d], sky=lax.rem(sky + d, ns))

    def ag_copy(d):
        return remote(part(pay_out, me), part(pay_out, me), ag_s.at[d], ag_r.at[me],
                      freq=lax.rem(me + d, nf))

    def ag_wait(d):
        q = lax.rem(me + nf - d, nf)
        remote(part(pay_out, q), part(pay_out, q), ag_s.at[0], ag_r.at[q], freq=q).wait_recv()

    for d in range(1, nf):
        rs_copy(d).start()
    dup.wait_recv()
    ddown.wait_recv()
    b = bw[...].astype(BF)

    def light(f):
        x = dr[f]
        rolled = dot(x, shift).astype(BF)
        full = jnp.concatenate([rolled[:, 128:256], x, rolled[:, 0:128]], axis=0)
        dl_ref[f] = dot(b, full).astype(BF)

    for f in range(F // 2):
        light(f)
    total = pay[pl.ds(pl.multiple_of(me * rows, 8), rows), :]
    for d in range(1, nf):
        rs_copy(d).wait_recv()
        total = total + rs[d]
    own[...] = total
    for d in range(1, ns):
        sk_copy(d).start()
    for f in range(F // 2, F):
        light(f)
    for d in range(1, ns):
        sk_copy(d).wait_recv()
        total = total + sk[d]
    pay_out[pl.ds(pl.multiple_of(me * rows, 8), rows), :] = total
    for d in range(1, nf):
        ag_copy(d).start()
    for d in range(1, nf):
        ag_wait(d)

    up.wait_send()
    down.wait_send()
    dup.wait_send()
    ddown.wait_send()
    for d in range(1, nf):
        rs_copy(d).wait_send()
        ag_copy(d).wait_send()

        @pl.when(me >= d)
        def _():
            dec_copy(d).wait_send()
    for d in range(1, ns):
        sk_copy(d).wait_send()
    for h in range(2):
        for d in range(1, chips):
            @pl.when(chip >= d)
            def _():
                cot_copy(d, h).wait_send()

            @pl.when(chip + d < chips)
            def _():
                fwd_copy(d, h).wait_send()

        @pl.when(core == 1)
        def _():
            sib_copy(h).wait_send()


def finish(scale, dl_ref, pay_ref, in_ref, out_ref, dl_out, conv_out, din_out, dout_out, skip_out):
    dl_out[...] = dl_ref[...]
    for dr in range(3):
        for k in range(3):
            at = (dr * 3 + k) * 32
            conv_out[:, at:at + 32] = pay_ref[k * 32:(k + 1) * 32, dr * 32:(dr + 1) * 32] * scale
    t = jnp.concatenate([pay_ref[96 + k:97 + k, :] for k in range(4)], axis=1) * scale
    t = jnp.where(lax.rem(iota((16, 512), 1), 16) == iota((16, 512), 0), t, 0.0)
    join = (iota((512, 32), 0) // 16 == iota((512, 32), 1)).astype(F32)
    t = jnp.dot(t, join, precision=lax.Precision.HIGHEST, preferred_element_type=F32)
    din_out[...] = t * out_ref[...]
    dout_out[...] = t * in_ref[...]
    s = pay_ref[100:101, :] * scale
    skip_out[...] = s[:, 0:32] + s[:, 32:64] + s[:, 64:96] + s[:, 96:128]


def per_device(lightcone, cotangent, conv_weight, in_proj, out_proj, skip_gain, decay):
    F, C, R, W = lightcone.shape
    N = in_proj.shape[1]
    nf, ns = lax.axis_size("freq"), lax.axis_size("sky")
    scale = 1.0 / float(F * nf * R * ns * W) ** 0.5
    rows = 128 // nf
    dma = pltpu.SemaphoreType.DMA
    vm = pl.BlockSpec(memory_space=pltpu.VMEM)
    dl, pay = pl.pallas_call(
        functools.partial(kernel, nf, ns),
        out_shape=(
            jax.ShapeDtypeStruct((F, C * R, W), BF),
            jax.ShapeDtypeStruct((128, 128), F32),
        ),
        in_specs=[pl.BlockSpec(memory_space=pltpu.MemorySpace.HBM)] * 7,
        out_specs=(vm, vm),
        scratch_shapes=[
            pltpu.VMEM((F, 4 * C, W), BF),
            pltpu.VMEM((nf, R, F * C, W), BF),
            pltpu.VMEM((nf, F, C * N), F32),
            pltpu.VMEM((F * C, R * W), BF),
            pltpu.VMEM((nf, 4 * F, 4 * C * N), F32),
            pltpu.VMEM((F, C * N), F32),
            pltpu.VMEM((4 * F, 128), F32),
            pltpu.VMEM((4 * F, 128), F32),
            pltpu.VMEM((nf, F * C, F * C), BF),
            pltpu.VMEM((F, 4 * C, W), BF),
            pltpu.VMEM((8, 4 * C * N), F32),
            pltpu.VMEM((128, 128), F32),
            pltpu.VMEM((nf, rows, 128), F32),
            pltpu.VMEM((ns, rows, 128), F32),
            pltpu.VMEM((rows, 128), F32),
            pltpu.VMEM((2 * C, 12 * C), BF),
            pltpu.VMEM((2 * C, 12 * C), F32),
            dma((2,)), dma((2,)), dma((2,)), dma((2,)),
            dma((nf,)), dma((nf,)), dma((nf, 2)), dma((nf, 2)), dma((nf, 2)),
            dma((nf,)), dma((nf,)), dma((ns,)), dma((ns,)), dma((nf,)), dma((nf,)),
            pltpu.VMEM((F, C * R, W), BF),
            pltpu.VMEM((F, C * R, W), BF),
            pltpu.VMEM((C, 9 * C), BF),
            pltpu.VMEM((N, C), F32),
            pltpu.VMEM((N, C), F32),
            pltpu.VMEM((1, C), F32),
            dma((7,)),
        ],
        compiler_params=pltpu.CompilerParams(
            collective_id=0, has_side_effects=True, vmem_limit_bytes=63 << 20),
    )(lightcone.reshape(F, C * R, W), cotangent.reshape(F, C * R, W), conv_weight,
      in_proj.T, out_proj.T, skip_gain.reshape(1, C), decay)
    dl, grad, din, dout, d_skip = pl.pallas_call(
        functools.partial(finish, scale),
        out_shape=(
            jax.ShapeDtypeStruct((F, C * R, W), BF),
            jax.ShapeDtypeStruct((C, 9 * C), F32),
            jax.ShapeDtypeStruct((N, C), F32),
            jax.ShapeDtypeStruct((N, C), F32),
            jax.ShapeDtypeStruct((1, C), F32),
        ),
        in_specs=[vm] * 4,
        out_specs=(vm,) * 5,
        compiler_params=pltpu.CompilerParams(vmem_limit_bytes=63 << 20),
    )(dl, pay, in_proj.T, out_proj.T)
    return dl.reshape(F, C, R, W), grad, din.T, dout.T, d_skip.reshape(C)


def solution(mesh):
    return jax.shard_map(
        per_device,
        mesh=mesh,
        in_specs=(
            P(("replica", "freq"), None, "sky", None),
            P(("replica", "freq"), None, "sky", None),
            P(),
            P(),
            P(),
            P(),
            P("freq", None),
        ),
        out_specs=(
            P(("replica", "freq"), None, "sky", None),
            P("replica", None),
            P("replica", None),
            P("replica", None),
            P("replica"),
        ),
        check_vma=False,
    )
```
